32 devices in a mesh: pair: 8 (over y, x, core), grp: 4 (over z).
Axes of the slice: x: 2, y: 2, z: 4, core: 2. Of those that a mesh axis runs over, the one named last changes fastest.
Arguments:
- amplitudes: float32 [64, 64, 4096], P('pair'), may hold values from -6 to 6
- integrals: float32 [4, 8, 4, 64, 4096], P('grp', 'pair'), may hold values from -0.09375 to 0.09375
- tasks: int32 [4, 8, 4], P('grp', 'pair'), may hold values from -1 to 63, as said below
Outputs:
- residual: float32 [4, 512, 64], P('grp', 'pair')
The draws below stay inside these ranges and needn't reach their ends.
Inputs may be any that keep to these rules, and one draw needn't show every extreme that they name: `tasks`: in each device's list the live entries (not -1) come first and are distinct; every device has at least one live entry, and in every index of grp some device has all 4 live.
All inputs are finite; a program needn't handle non-finite values.
Results may differ from the reference program's by a relative error of at most 0.0003.
Values sent between devices are 32-bit elements; how exact they have to be, the bound alone decides.
A program may use at most 128 MiB of HBM per device.

```python
import jax
import jax.numpy as jnp
from jax import lax

TS = 64
NT = 8
SLOT_DEV = 4
NCD = 64
PAIRS = 64
N_PAIR = 8
N_GRP = 4


def draw_tasks(key, part):
    choice_count = NT * (NT * NT // N_PAIR)
    key_count, key_full, key_perm = jax.random.split(key, 3)
    counts = jax.random.randint(key_count, (N_GRP, N_PAIR), 1, SLOT_DEV + 1)
    full_device = jax.random.randint(key_full, (N_GRP,), 0, N_PAIR)
    counts = jnp.where(jnp.arange(N_PAIR)[None, :] == full_device[:, None], SLOT_DEV, counts)
    perm_keys = jax.random.split(key_perm, N_GRP * N_PAIR)
    picked = jax.vmap(lambda single: jax.random.permutation(single, choice_count)[:SLOT_DEV])(perm_keys)
    picked = picked.reshape(N_GRP, N_PAIR, SLOT_DEV)
    filled = jnp.arange(SLOT_DEV)[None, None, :] < counts[..., None]
    return jnp.where(filled, picked, -1).astype(jnp.int32)


def levels(own_key, dims, cuts, low, top_value):
    gain = 1.0
    for axis_at, blocks in cuts:
        heights = jax.random.uniform(jax.random.fold_in(jax.random.fold_in(own_key, 6), axis_at), (blocks,), jnp.float32, low / len(cuts), top_value / len(cuts))
        gain = gain * jnp.repeat(jnp.exp(heights), dims[axis_at] // blocks).reshape((-1,) + (1,) * (len(dims) - 1 - axis_at))
    return gain


def bell_draw(rng, shape, width, limit, cuts=(), kind=jnp.bfloat16):
    array = width * jax.random.normal(rng, shape, jnp.float32)
    if cuts:
        array = array * levels(rng, shape, cuts, -0.22, 0.18)
    return jnp.clip(array, -limit, limit).astype(kind)


def setup_inputs(seed: int = 0) -> dict:
    seeds = jax.random.split(jax.random.key(seed), 4)
    return {
        "amplitudes": bell_draw(seeds[0], (PAIRS, NCD, TS * TS), 1.0, 6.0, ((0, 8),), jnp.float32),
        "integrals": bell_draw(seeds[1], (N_GRP, N_PAIR, SLOT_DEV, TS, TS * TS), (TS * TS) ** -0.5, 0.09375, ((0, 4), (1, 8)), jnp.float32),
        "tasks": draw_tasks(jax.random.fold_in(seeds[3], 71), 0),
    }


def reference(amplitudes, integrals, tasks):
    local_pairs = NT * NT // N_PAIR

    def one_group(group_args):
        blocks, codes = group_args
        valid = codes >= 0
        safe = jnp.maximum(codes, 0)
        column = jnp.arange(N_PAIR, dtype=jnp.int32)[:, None] * local_pairs + safe % local_pairs
        chosen = amplitudes[:, column, :]
        contrib = jnp.einsum("qkrc,pqkc->qkrp", blocks, chosen, precision=lax.Precision.HIGHEST)
        onehot = ((safe // local_pairs)[..., None] == jnp.arange(NT, dtype=jnp.int32)) & valid[..., None]
        onehot = onehot.astype(jnp.float32)
        total = jnp.einsum("qkb,qkrp->brp", onehot, contrib, precision=lax.Precision.HIGHEST)
        return total.reshape(NT * TS, PAIRS)

    return lax.map(one_group, (integrals, tasks))
```

```python
import functools

import jax
import jax.numpy as jnp
from jax import lax
from jax.experimental import pallas as pl
from jax.experimental.pallas import tpu as pltpu
from jax.sharding import PartitionSpec as P

NT = 8
MESH = pl.DeviceIdType.MESH


def split(x):
    high = x.astype(jnp.bfloat16)
    low = (x - high.astype(jnp.float32)).astype(jnp.bfloat16)
    return jnp.concatenate([high, low], axis=0)


def kernel(n, columns, tasks_ref, amp_ref, int_ref, out_ref, listed, amp, blocks, sent, held, total, parts,
           local_sem, list_send, list_recv, send_sem, recv_sem, part_send, part_recv):
    me = lax.axis_index("pair")
    grp = lax.axis_index("grp")
    own_rows, pairs, depth = amp_ref.shape
    slots, width, _ = int_ref.shape
    local = pairs // n
    part_rows = out_ref.shape[0]
    lists = columns < local

    load_amp = pltpu.make_async_copy(amp_ref, amp, local_sem.at[0])
    load_int = pltpu.make_async_copy(int_ref, blocks, local_sem.at[1])
    load_amp.start()
    load_int.start()

    def other(d):
        return lax.rem(me + d, n)

    def target(p):
        return (p, grp)

    barrier = pltpu.get_barrier_semaphore()

    @pl.loop(1, n)
    def _(d):
        pl.semaphore_signal(barrier, inc=1, device_id=target(other(d)), device_id_type=MESH)

    pl.semaphore_wait(barrier, n - 1)

    def list_copy(frm, to):
        return pltpu.make_async_remote_copy(
            src_ref=tasks_ref, dst_ref=listed.at[frm], send_sem=list_send.at[to], recv_sem=list_recv.at[frm],
            device_id=target(to), device_id_type=MESH)

    def column_copy(c, frm, to):
        return pltpu.make_async_remote_copy(
            src_ref=sent.at[c, to], dst_ref=held.at[c, frm], send_sem=send_sem.at[c, to],
            recv_sem=recv_sem.at[c, frm], device_id=target(to), device_id_type=MESH)

    def part_copy(frm, to):
        return pltpu.make_async_remote_copy(
            src_ref=total.at[to], dst_ref=parts.at[frm], send_sem=part_send.at[to],
            recv_sem=part_recv.at[frm], device_id=target(to), device_id_type=MESH)

    if lists:
        @pl.loop(1, n)
        def _(d):
            list_copy(me, other(d)).start()

        @pl.loop(1, n)
        def _(d):
            list_copy(other(d), other(d)).wait_recv()

    load_amp.wait()

    def column(p, c, codes):
        if lists:
            return p * local + lax.rem(jnp.maximum(codes(c), 0), local)
        return p * local + c

    for c in range(columns):
        @pl.loop(1, n)
        def _(d):
            p = other(d)
            at = column(p, c, lambda k: listed[p, 0, k])
            for row in range(own_rows):
                sent[c, p, pl.ds(row, 1), :] = amp[row, pl.ds(at, 1), :]

            @pl.when(d > 1)
            def _():
                column_copy(c, me, other(d - 1)).start()

        at = column(me, c, lambda k: tasks_ref[0, k])
        for row in range(own_rows):
            held[c, me, pl.ds(row, 1), :] = amp[row, pl.ds(at, 1), :]
        column_copy(c, me, other(n - 1)).start()

    load_int.wait()
    total[...] = jnp.zeros_like(total)

    def arrive(c):
        @pl.loop(1, n)
        def _(d):
            column_copy(c, other(d), other(d)).wait_recv()

    if not lists:
        for c in range(columns):
            arrive(c)

    @pl.loop(0, slots)
    def _(slot):
        code = tasks_ref[0, slot]
        safe = jnp.maximum(code, 0)
        if lists:
            arrive(slot)
            chosen = held[slot]
        else:
            chosen = held[lax.rem(safe, local)]
        chosen = chosen.reshape(n * own_rows, depth)
        rows = split(blocks[slot])
        both = lax.dot_general(rows, split(chosen), (((1,), (1,)), ((), ())), preferred_element_type=jnp.float32)
        both = both[:width] + both[width:]
        term = both[:, : n * own_rows] + both[:, n * own_rows:]
        tile = jnp.where(code >= 0, lax.div(safe, local), -1)
        for p in range(n):
            first = p * part_rows
            total[p] += jnp.where(tile == first // width, term[first % width: first % width + part_rows], 0.0)

    @pl.loop(1, n)
    def _(d):
        part_copy(me, other(d)).start()

    parts[me] = total[me]

    @pl.loop(1, n)
    def _(d):
        part_copy(other(d), other(d)).wait_recv()

    result = parts[0]
    for p in range(1, n):
        result += parts[p]
    out_ref[...] = result

    @pl.loop(1, n)
    def _(d):
        part_copy(me, other(d)).wait_send()
        if lists:
            list_copy(me, other(d)).wait_send()
        for c in range(columns):
            column_copy(c, me, other(d)).wait_send()


def body(n, amplitudes, integrals, tasks):
    own_rows, pairs, depth = amplitudes.shape
    slots, width = integrals.shape[2:4]
    local = pairs // n
    columns = min(local, slots)
    part_rows = NT * width // n
    out = pl.pallas_call(
        functools.partial(kernel, n, columns),
        out_shape=jax.ShapeDtypeStruct((part_rows, n * own_rows), jnp.float32),
        in_specs=[
            pl.BlockSpec(memory_space=pltpu.SMEM),
            pl.BlockSpec(memory_space=pl.ANY),
            pl.BlockSpec(memory_space=pl.ANY),
        ],
        out_specs=pl.BlockSpec(memory_space=pltpu.VMEM),
        scratch_shapes=[
            pltpu.SMEM((n, 1, slots), jnp.int32),
            pltpu.VMEM(amplitudes.shape, jnp.float32),
            pltpu.VMEM((slots, width, depth), jnp.float32),
            pltpu.VMEM((columns, n, own_rows, depth), jnp.float32),
            pltpu.VMEM((columns, n, own_rows, depth), jnp.float32),
            pltpu.VMEM((n, part_rows, n * own_rows), jnp.float32),
            pltpu.VMEM((n, part_rows, n * own_rows), jnp.float32),
            pltpu.SemaphoreType.DMA((2,)),
            pltpu.SemaphoreType.DMA((n,)),
            pltpu.SemaphoreType.DMA((n,)),
            pltpu.SemaphoreType.DMA((columns, n)),
            pltpu.SemaphoreType.DMA((columns, n)),
            pltpu.SemaphoreType.DMA((n,)),
            pltpu.SemaphoreType.DMA((n,)),
        ],
        compiler_params=pltpu.CompilerParams(
            collective_id=0, has_side_effects=True, vmem_limit_bytes=60 * 1024 * 1024),
    )(tasks[0], amplitudes, integrals[0, 0])
    return out[None]


def solution(mesh):
    return jax.shard_map(
        functools.partial(body, mesh.shape["pair"]),
        mesh=mesh,
        in_specs=(
            P("pair", None, None),
            P("grp", "pair", None, None, None),
            P("grp", "pair", None),
        ),
        out_specs=P("grp", "pair", None),
        check_vma=False,
    )
```

```python
import functools

import jax
import jax.numpy as jnp
from jax import lax
from jax.experimental import pallas as pl
from jax.experimental.pallas import tpu as pltpu
from jax.sharding import PartitionSpec as P

NT = 8
SHARED = 896
MESH = pl.DeviceIdType.MESH


def split(x):
    high = x.astype(jnp.bfloat16)
    low = (x - high.astype(jnp.float32)).astype(jnp.bfloat16)
    return jnp.concatenate([high, low], axis=0)


def kernel(n, layers, columns, shared, pack, tasks_ref, amp_ref, int_ref, out_ref, listed, amp, blocks, rows, sent,
           held, sent_shared, held_shared, total, parts, local_sem, list_send, list_recv, send_sem, recv_sem,
           fetch_send, fetch_recv, layer_send, layer_recv, part_send, part_recv):
    me = lax.axis_index("pair")
    grp = lax.axis_index("grp")
    own_rows, pairs, depth = amp_ref.shape
    slots, width, _ = int_ref.shape
    local = pairs // n
    per = local // layers if shared else 1
    part_rows = out_ref.shape[0]
    lists = columns < local
    tail = pl.ds(shared, depth - shared)

    load_amp = pltpu.make_async_copy(amp_ref, amp, local_sem.at[0])
    load_int = pltpu.make_async_copy(int_ref, blocks, local_sem.at[1])
    load_amp.start()
    load_int.start()

    def other(d):
        return lax.rem(me + d, n)

    def target(p):
        return (p, grp)

    barrier = pltpu.get_barrier_semaphore()

    @pl.loop(1, n)
    def _(d):
        pl.semaphore_signal(barrier, inc=1, device_id=target(other(d)), device_id_type=MESH)

    if shared:
        @pl.when(grp > 0)
        def _():
            pl.semaphore_signal(barrier, inc=1, device_id=(me, grp - 1), device_id_type=MESH)

        @pl.when(grp < layers - 1)
        def _():
            pl.semaphore_signal(barrier, inc=1, device_id=(me, grp + 1), device_id_type=MESH)

        peers = n - 1 + jnp.minimum(grp, 1) + jnp.minimum(layers - 1 - grp, 1)
        pl.semaphore_wait(barrier, peers)
    else:
        pl.semaphore_wait(barrier, n - 1)

    def list_copy(frm, to):
        return pltpu.make_async_remote_copy(
            src_ref=tasks_ref, dst_ref=listed.at[frm], send_sem=list_send.at[to], recv_sem=list_recv.at[frm],
            device_id=target(to), device_id_type=MESH)

    def column_copy(c, frm, to):
        return pltpu.make_async_remote_copy(
            src_ref=sent.at[c, to], dst_ref=held.at[c, frm], send_sem=send_sem.at[c, to],
            recv_sem=recv_sem.at[c, frm], device_id=target(to), device_id_type=MESH)

    def fetch_copy(j, frm, to):
        return pltpu.make_async_remote_copy(
            src_ref=sent_shared.at[j, to], dst_ref=held_shared.at[grp * per + j, frm],
            send_sem=fetch_send.at[j, to], recv_sem=fetch_recv.at[j, frm], device_id=target(to), device_id_type=MESH)

    def layer_copy(block, j, step):
        at = held_shared.at[block * per + j]
        return pltpu.make_async_remote_copy(
            src_ref=at, dst_ref=at, send_sem=layer_send.at[(step + 1) // 2, block * per + j],
            recv_sem=layer_recv.at[block * per + j], device_id=(me, grp + step), device_id_type=MESH)

    def part_copy(frm, to):
        return pltpu.make_async_remote_copy(
            src_ref=total.at[to], dst_ref=parts.at[frm], send_sem=part_send.at[to],
            recv_sem=part_recv.at[frm], device_id=target(to), device_id_type=MESH)

    if lists:
        @pl.loop(1, n)
        def _(d):
            list_copy(me, other(d)).start()

    load_amp.wait()

    if shared:
        for j in range(per):
            @pl.loop(1, n)
            def _(d):
                p = other(d)
                for row in range(own_rows):
                    sent_shared[j, p, pl.ds(row, 1), :] = amp[
                        row, pl.ds(p * local + grp * per + j, 1), pl.ds(0, shared)]

                @pl.when(d > 1)
                def _():
                    fetch_copy(j, me, other(d - 1)).start()

            for row in range(own_rows):
                held_shared[grp * per + j, me, pl.ds(row, 1), :] = amp[
                    row, pl.ds(me * local + grp * per + j, 1), pl.ds(0, shared)]
            fetch_copy(j, me, other(n - 1)).start()

    if lists:
        @pl.loop(1, n)
        def _(d):
            list_copy(other(d), other(d)).wait_recv()

    def column(p, c, codes):
        if lists:
            return p * local + lax.rem(jnp.maximum(codes(c), 0), local)
        return p * local + c

    for c in range(columns):
        @pl.loop(1, n)
        def _(d):
            p = other(d)
            at = column(p, c, lambda k: listed[p, 0, k])
            for row in range(own_rows):
                sent[c, p, pl.ds(row, 1), :] = amp[row, pl.ds(at, 1), tail]

            @pl.when(d > 1)
            def _():
                column_copy(c, me, other(d - 1)).start()

        at = column(me, c, lambda k: tasks_ref[0, k])
        for row in range(own_rows):
            held[c, me, pl.ds(row, 1), :] = amp[row, pl.ds(at, 1), tail]
        column_copy(c, me, other(n - 1)).start()

    def forward(hop, j, act):
        @pl.when((grp - hop >= 0) & (grp + 1 < layers))
        def _():
            act(layer_copy(grp - hop, j, 1))

        @pl.when((grp + hop < layers) & (grp >= 1))
        def _():
            act(layer_copy(grp + hop, j, -1))

    def stage(hop):
        for j in range(per):
            @pl.when(grp - hop >= 0)
            def _():
                layer_copy(grp - hop, j, 1).wait_recv()

            @pl.when(grp + hop < layers)
            def _():
                layer_copy(grp + hop, j, -1).wait_recv()

            if hop < layers - 1:
                forward(hop, j, lambda copy: copy.start())

    load_int.wait()

    @pl.loop(0, slots)
    def _(slot):
        rows[slot] = split(blocks[slot])

    total[...] = jnp.zeros_like(total)

    if shared:
        for j in range(per):
            @pl.loop(1, n)
            def _(d):
                fetch_copy(j, other(d), other(d)).wait_recv()

            forward(0, j, lambda copy: copy.start())

    def arrive(c):
        @pl.loop(1, n)
        def _(d):
            column_copy(c, other(d), other(d)).wait_recv()

    def add(slot, chosen, span):
        code = tasks_ref[0, slot]
        chosen = chosen.reshape(n * own_rows, chosen.shape[-1])
        both = lax.dot_general(rows[slot, :, span], split(chosen), (((1,), (1,)), ((), ())),
                               preferred_element_type=jnp.float32)
        both = both[:width] + both[width:]
        term = both[:, : n * own_rows] + both[:, n * own_rows:]
        tile = jnp.where(code >= 0, lax.div(jnp.maximum(code, 0), local), -1)
        piece = part_rows // pack
        packed = {}
        for p in range(n):
            first = p * part_rows
            low = first % width
            if low not in packed:
                packed[low] = jnp.concatenate(
                    [term[low + i * piece: low + (i + 1) * piece] for i in range(pack)], axis=1)
            total[p] += jnp.where(tile == first // width, packed[low], 0.0)

    def picked(slot):
        return lax.rem(jnp.maximum(tasks_ref[0, slot], 0), local)

    if lists:
        for slot in range(slots):
            if shared:
                for hop in range(slot + 1, layers if slot == slots - 1 else min(slot + 2, layers)):
                    stage(hop)
            if shared and slot == slots - 1:
                @pl.loop(0, slots)
                def _(each):
                    add(each, held_shared[picked(each)], pl.ds(0, shared))

            arrive(slot)
            add(slot, held[slot], tail)
    else:
        for c in range(columns):
            arrive(c)

        @pl.loop(0, slots)
        def _(slot):
            add(slot, held[picked(slot)], tail)

    @pl.loop(1, n)
    def _(d):
        part_copy(me, other(d)).start()

    parts[me] = total[me]

    @pl.loop(1, n)
    def _(d):
        part_copy(other(d), other(d)).wait_recv()

    result = parts[0]
    for p in range(1, n):
        result += parts[p]
    piece = part_rows // pack
    for i in range(pack):
        out_ref[i * piece: (i + 1) * piece, :] = result[:, i * n * own_rows: (i + 1) * n * own_rows]

    if shared:
        for hop in range(layers - 1):
            for j in range(per):
                forward(hop, j, lambda copy: copy.wait_send())

    @pl.loop(1, n)
    def _(d):
        part_copy(me, other(d)).wait_send()
        if lists:
            list_copy(me, other(d)).wait_send()
        if shared:
            for j in range(per):
                fetch_copy(j, me, other(d)).wait_send()
        for c in range(columns):
            column_copy(c, me, other(d)).wait_send()


def body(n, layers, amplitudes, integrals, tasks):
    own_rows, pairs, depth = amplitudes.shape
    slots, width = integrals.shape[2:4]
    local = pairs // n
    columns = min(local, slots)
    part_rows = NT * width // n
    held_rows = n * own_rows
    pack = max(1, 128 // held_rows)
    shared = SHARED if columns < local and local % layers == 0 else 0
    per = local // layers if shared else 1
    span = max(shared, 128)
    heads = n if shared else 1
    out = pl.pallas_call(
        functools.partial(kernel, n, layers, columns, shared, pack),
        out_shape=jax.ShapeDtypeStruct((part_rows, held_rows), jnp.float32),
        in_specs=[
            pl.BlockSpec(memory_space=pltpu.SMEM),
            pl.BlockSpec(memory_space=pl.ANY),
            pl.BlockSpec(memory_space=pl.ANY),
        ],
        out_specs=pl.BlockSpec(memory_space=pltpu.VMEM),
        scratch_shapes=[
            pltpu.SMEM((n, 1, slots), jnp.int32),
            pltpu.VMEM(amplitudes.shape, jnp.float32),
            pltpu.VMEM((slots, width, depth), jnp.float32),
            pltpu.VMEM((slots, 2 * width, depth), jnp.bfloat16),
            pltpu.VMEM((columns, n, own_rows, depth - shared), jnp.float32),
            pltpu.VMEM((columns, n, own_rows, depth - shared), jnp.float32),
            pltpu.VMEM((per, heads, own_rows, span), jnp.float32),
            pltpu.VMEM((local, heads, own_rows, span), jnp.float32),
            pltpu.VMEM((n, part_rows // pack, held_rows * pack), jnp.float32),
            pltpu.VMEM((n, part_rows // pack, held_rows * pack), jnp.float32),
            pltpu.SemaphoreType.DMA((2,)),
            pltpu.SemaphoreType.DMA((n,)),
            pltpu.SemaphoreType.DMA((n,)),
            pltpu.SemaphoreType.DMA((columns, n)),
            pltpu.SemaphoreType.DMA((columns, n)),
            pltpu.SemaphoreType.DMA((per, n)),
            pltpu.SemaphoreType.DMA((per, n)),
            pltpu.SemaphoreType.DMA((2, local)),
            pltpu.SemaphoreType.DMA((local,)),
            pltpu.SemaphoreType.DMA((n,)),
            pltpu.SemaphoreType.DMA((n,)),
        ],
        compiler_params=pltpu.CompilerParams(
            collective_id=0, has_side_effects=True, vmem_limit_bytes=60 * 1024 * 1024),
    )(tasks[0], amplitudes, integrals[0, 0])
    return out[None]


def solution(mesh):
    return jax.shard_map(
        functools.partial(body, mesh.shape["pair"], mesh.shape["grp"]),
        mesh=mesh,
        in_specs=(
            P("pair", None, None),
            P("grp", "pair", None, None, None),
            P("grp", "pair", None),
        ),
        out_specs=P("grp", "pair", None),
        check_vma=False,
    )
```
